32 devices in a mesh: tm: 4 (over y, x), region: 8 (over z, core).
Axes of the slice: x: 2, y: 2, z: 4, core: 2. Of those that a mesh axis runs over, the one named last changes fastest.
Arguments:
- gen: float32 [8, 128, 4, 128], P('region', None, 'tm'), may hold values from 0 to 1
- flow: float32 [32, 128, 4, 128], P('region', None, 'tm'), may hold values from -4 to 4
- price: float32 [32, 128, 4, 128], P('region', None, 'tm'), may hold values from -6 to 6
- ramp_dual: float32 [8, 128, 4, 128], P('region', None, 'tm'), may hold values from -3 to 3
- demand: float32 [32, 128, 4, 128], P('region', None, 'tm'), may hold values from -6 to 6
- incid_tiles: bfloat16 [256, 128, 128], P('region'), may hold values from -0.1875 to 0.1875
- tile_bus: int32 [256], P('region'), may hold values from 0 to 3
- tile_line: int32 [256], P('region'), may hold values from 0 to 31, as said below
- gen_tiles: bfloat16 [8, 128, 128], P('region'), may hold values from -0.5 to 0.5
- gen_bus: int32 [8], P('region'), may hold values from 0 to 3
- gen_cost: float32 [8, 128], P('region'), may hold values from 0.1 to 1
- gen_cap: float32 [8, 128], P('region'), may hold values from 0.5 to 2
- ramp_cap: float32 [8, 128], P('region'), may hold values from 0.05 to 0.5
- flow_cap: float32 [32, 128], P('region'), may hold values from 0.3 to 1.5
- weight: float32 [], replicated, may hold values from 0.5 to 2
Outputs:
- gen_next: float32 [8, 128, 4, 128], P('region', None, 'tm')
- flow_next: float32 [32, 128, 4, 128], P('region', None, 'tm')
- price_next: float32 [32, 128, 4, 128], P('region', None, 'tm')
- ramp_next: float32 [8, 128, 4, 128], P('region', None, 'tm')
The draws below stay inside these ranges and needn't reach their ends.
Inputs may be any that keep to these rules, and one draw needn't show every extreme that they name: Tile t belongs to region r = t // 32; its line block lies in region r - 1, r or r + 1 (those that exist), where region q holds line blocks q * 4 to (q + 1) * 4 - 1. No two tiles have the same pair (tile_bus, tile_line) within a region.
All inputs are finite; a program needn't handle non-finite values.
Results may differ from the reference program's by a relative error of at most 0.0006.
The reference program's roundings to bfloat16 on the way (of `price_low`) count: a program that leaves them out, or rounds other values in their place, can miss the bound.
Values may be sent and summed in bfloat16 or wider, within the bound.
A program may use at most 64 MiB of HBM per device.

```python
import math
import jax
import jax.numpy as jnp
from jax import lax

BLK = 128
S = 128
BUS_BLK_DEV = 4
LINE_BLK_DEV = 4
GEN_BLK_DEV = 1
TILE_DEV = 32
HOURS = 4
BUS_BLKS = 32
LINE_BLKS = 32
GEN_BLKS = 8
TILES = 256


def tile_positions(key):
    regions = LINE_BLKS // LINE_BLK_DEV
    slots = BUS_BLK_DEV * 3 * LINE_BLK_DEV
    base = jax.random.fold_in(key, 7)
    region_keys = jax.random.split(base, regions)
    perms = jax.vmap(lambda one: jax.random.permutation(one, slots))(region_keys).astype(jnp.int32)
    window = perms // BUS_BLK_DEV
    buses = perms % BUS_BLK_DEV
    region = jnp.arange(regions, dtype=jnp.int32)[:, None]
    lines = (region - 1) * LINE_BLK_DEV + window
    valid = (lines >= 0) & (lines < LINE_BLKS)
    order_key = jnp.where(valid, 0, slots).astype(jnp.int32) + jnp.arange(slots, dtype=jnp.int32)[None, :]
    order = jnp.argsort(order_key, axis=1)[:, :TILE_DEV]
    chosen_lines = jnp.take_along_axis(lines, order, axis=1)
    chosen_buses = jnp.take_along_axis(buses, order, axis=1)
    return (chosen_buses.reshape(-1).astype(jnp.int32), chosen_lines.reshape(-1).astype(jnp.int32))


def draw_tile_bus(key, part):
    buses, lines = tile_positions(key)
    return buses


def draw_tile_line(key, part):
    buses, lines = tile_positions(key)
    return lines


def set_ends(result, stream_key, low, high):
    spot = [jax.random.randint(jax.random.fold_in(stream_key, axis), (), 0, length) for axis, length in enumerate(result.shape)]
    main_axis = result.shape.index(max(result.shape))
    next_to = spot[:main_axis] + [(spot[main_axis] + 1) % result.shape[main_axis]] + spot[main_axis + 1:]
    return result.at[tuple(spot)].set(low).at[tuple(next_to)].set(high)


def steps_of(stream_key, dims, pieces, smallest, top_value):
    level, own = 1.0, jax.random.fold_in(stream_key, 6)
    for axis_at, blocks in pieces:
        steps = jnp.exp(jax.random.uniform(jax.random.fold_in(own, axis_at), (blocks,), jnp.float32, smallest / len(pieces), top_value / len(pieces)))
        level = level * jnp.repeat(steps, dims[axis_at] // blocks).reshape([-1 if axis == axis_at else 1 for axis in range(len(dims))])
    return level


def noise(rng, extent, scale, most, pieces=(), held_as=jnp.bfloat16):
    values = jax.random.normal(rng, extent, jnp.float32) * scale
    if len(pieces) > 0:
        values = steps_of(rng, extent, pieces, -0.22, 0.18) * values
    return jnp.clip(values, min=-most, max=most).astype(held_as)


def setup_inputs(seed: int = 0) -> dict:
    key_list = jax.random.split(jax.random.key(seed), 16)
    return {
        "gen": jnp.clip(1.0 * jax.random.uniform(key_list[0], (GEN_BLKS, BLK, HOURS, S), jnp.float32) ** steps_of(key_list[0], (GEN_BLKS, BLK, HOURS, S), ((0, 8), (2, 4)), -0.2, 0.2), 0.0, 1.0),
        "flow": noise(key_list[1], (LINE_BLKS, BLK, HOURS, S), 0.5, 4.0, ((0, 8), (2, 4)), jnp.float32),
        "price": noise(key_list[2], (BUS_BLKS, BLK, HOURS, S), 1.0, 6.0, ((0, 8), (2, 4)), jnp.float32),
        "ramp_dual": noise(key_list[3], (GEN_BLKS, BLK, HOURS, S), 0.3, 3.0, ((0, 8), (2, 4)), jnp.float32),
        "demand": noise(key_list[4], (BUS_BLKS, BLK, HOURS, S), 1.0, 6.0, ((0, 8), (2, 4)), jnp.float32),
        "incid_tiles": noise(key_list[5], (TILES, BLK, BLK), (TILE_DEV // BUS_BLK_DEV * BLK + BLK) ** -0.5, 0.1875, ((0, 8),)),
        "tile_bus": draw_tile_bus(jax.random.fold_in(key_list[15], 71), 0),
        "tile_line": draw_tile_line(jax.random.fold_in(key_list[15], 71), 0),
        "gen_tiles": noise(key_list[8], (GEN_BLKS, BLK, BLK), BLK ** -0.5, 0.5, ((0, 8),)),
        "gen_bus": set_ends(jax.random.randint(key_list[9], (GEN_BLKS,), 0, BUS_BLK_DEV), jax.random.fold_in(key_list[9], 1), 0, BUS_BLK_DEV - 1).astype(jnp.int32),
        "gen_cost": jnp.clip(jnp.exp(math.log(1.0) - 2.3025851 * jax.random.uniform(key_list[10], (GEN_BLKS, BLK), jnp.float32) ** steps_of(key_list[10], (GEN_BLKS, BLK), ((0, 8),), -0.2, 0.2)), 0.1, 1.0),
        "gen_cap": jnp.clip(0.5 + 1.5 * jax.random.uniform(key_list[11], (GEN_BLKS, BLK), jnp.float32) ** steps_of(key_list[11], (GEN_BLKS, BLK), ((0, 8),), -0.2, 0.2), 0.5, 2.0),
        "ramp_cap": jnp.clip(jnp.exp(math.log(0.5) - 2.3025851 * jax.random.uniform(key_list[12], (GEN_BLKS, BLK), jnp.float32) ** steps_of(key_list[12], (GEN_BLKS, BLK), ((0, 8),), -0.2, 0.2)), 0.05, 0.5),
        "flow_cap": jnp.clip(0.3 + 1.2 * jax.random.uniform(key_list[13], (LINE_BLKS, BLK), jnp.float32) ** steps_of(key_list[13], (LINE_BLKS, BLK), ((0, 8),), -0.2, 0.2), 0.3, 1.5),
        "weight": jnp.clip(jnp.exp(jax.random.uniform(key_list[14], (), jnp.float32, math.log(0.5), math.log(2.0))), 0.5, 2.0),
    }


step_scale = 0.4
tiny = 1e-06

def push_buses(flow_low, gen_low, incid_tiles, tile_bus, tile_line, gen_tiles, gen_bus):
    regions = LINE_BLKS // LINE_BLK_DEV
    columns = HOURS * S
    flow_cols = flow_low.reshape(LINE_BLKS, BLK, columns)
    tiles_by = incid_tiles.reshape(regions, TILE_DEV, BLK, BLK)
    lines_by = tile_line.reshape(regions, TILE_DEV)
    buses_by = tile_bus.reshape(regions, TILE_DEV)

    def per_region(packed):
        tiles_here, lines_here, buses_here = packed
        picked = flow_cols[lines_here].astype(jnp.float32)
        contrib = jnp.einsum('tij,tjc->tic', tiles_here.astype(jnp.float32), picked)
        return jax.ops.segment_sum(contrib, buses_here, num_segments=BUS_BLK_DEV)
    bus_sum = lax.map(per_region, (tiles_by, lines_by, buses_by)).reshape(BUS_BLKS, BLK, columns)
    gen_cols = gen_low.reshape(GEN_BLKS, BLK, columns).astype(jnp.float32)
    gen_contrib = jnp.einsum('gij,gjc->gic', gen_tiles.astype(jnp.float32), gen_cols)
    target = jnp.arange(GEN_BLKS, dtype=jnp.int32) // GEN_BLK_DEV * BUS_BLK_DEV + gen_bus
    bus_sum = bus_sum.at[target].add(gen_contrib)
    return bus_sum.reshape(BUS_BLKS, BLK, HOURS, S)

def pull_lines(price_low, incid_tiles, tile_bus, tile_line, gen_tiles, gen_bus):
    regions = LINE_BLKS // LINE_BLK_DEV
    columns = HOURS * S
    price_cols = price_low.reshape(BUS_BLKS, BLK, columns)
    tiles_by = incid_tiles.reshape(regions, TILE_DEV, BLK, BLK)
    lines_by = tile_line.reshape(regions, TILE_DEV)
    buses_by = tile_bus.reshape(regions, TILE_DEV)

    def per_region(total, packed):
        tiles_here, lines_here, buses_here, region = packed
        picked = price_cols[region * BUS_BLK_DEV + buses_here].astype(jnp.float32)
        contrib = jnp.einsum('tji,tjc->tic', tiles_here.astype(jnp.float32), picked)
        return (total.at[lines_here].add(contrib), None)
    start = jnp.zeros((LINE_BLKS, BLK, columns), jnp.float32)
    region_ids = jnp.arange(regions, dtype=jnp.int32)
    total, unused = lax.scan(per_region, start, (tiles_by, lines_by, buses_by, region_ids))
    target = jnp.arange(GEN_BLKS, dtype=jnp.int32) // GEN_BLK_DEV * BUS_BLK_DEV + gen_bus
    gen_picked = price_cols[target].astype(jnp.float32)
    gen_pull = jnp.einsum('gji,gjc->gic', gen_tiles.astype(jnp.float32), gen_picked)
    return (total.reshape(LINE_BLKS, BLK, HOURS, S), gen_pull.reshape(GEN_BLKS, BLK, HOURS, S))

def iterate(state, primal_weight, fixed):
    gen, flow, price, ramp_dual = state
    demand, incid_tiles, tile_bus, tile_line, gen_tiles, gen_bus, gen_cost, gen_cap, ramp_cap, flow_cap = fixed
    step_primal = step_scale / primal_weight
    step_dual = step_scale * primal_weight
    price_low = price.astype(jnp.bfloat16)
    pull_f, pull_g = pull_lines(price_low, incid_tiles, tile_bus, tile_line, gen_tiles, gen_bus)
    back = ramp_dual - jnp.roll(ramp_dual, -1, axis=2)
    grad_gen = gen_cost[:, :, None, None] - pull_g + back
    gen_new = jnp.clip(gen - step_primal * grad_gen, 0.0, gen_cap[:, :, None, None])
    limit = flow_cap[:, :, None, None]
    flow_new = jnp.clip(flow + step_primal * pull_f, -limit, limit)
    gen_bar = 2.0 * gen_new - gen
    flow_bar = 2.0 * flow_new - flow
    pushed = push_buses(flow_bar.astype(jnp.bfloat16), gen_bar.astype(jnp.bfloat16), incid_tiles, tile_bus, tile_line, gen_tiles, gen_bus)
    price_new = price + step_dual * (demand - pushed)
    ramping = gen_bar - jnp.roll(gen_bar, 1, axis=2)
    lifted = ramp_dual + step_dual * ramping
    bound = ramp_cap[:, :, None, None]
    ramp_new = lifted - step_dual * jnp.clip(lifted / step_dual, -bound, bound)
    return (gen_new, flow_new, price_new, ramp_new)

def reference(gen, flow, price, ramp_dual, demand, incid_tiles, tile_bus, tile_line, gen_tiles, gen_bus, gen_cost, gen_cap, ramp_cap, flow_cap, weight):
    fixed = (demand, incid_tiles, tile_bus, tile_line, gen_tiles, gen_bus, gen_cost, gen_cap, ramp_cap, flow_cap)
    first = iterate((gen, flow, price, ramp_dual), weight, fixed)
    primal_sq = jnp.sum((first[0] - gen) ** 2) + jnp.sum((first[1] - flow) ** 2)
    dual_sq = jnp.sum((first[2] - price) ** 2) + jnp.sum((first[3] - ramp_dual) ** 2)
    primal_mean = primal_sq / (gen.size + flow.size)
    dual_mean = dual_sq / (price.size + ramp_dual.size)
    weight_two = jnp.sqrt(weight * jnp.sqrt((dual_mean + tiny) / (primal_mean + tiny)))
    second = iterate(first, weight_two, fixed)
    return (second[0], second[1], second[2], second[3])
```

```python
import functools

import jax
import jax.numpy as jnp
from jax import lax
from jax.experimental import pallas as pl
from jax.experimental.pallas import tpu as pltpu
from jax.sharding import PartitionSpec as P

MESH = pl.DeviceIdType.MESH
step_scale = 0.4
tiny = 1e-06
f32 = jnp.float32
bf16 = jnp.bfloat16


def remote(src, dst, send_sem, recv_sem, axis, peer):
    return pltpu.make_async_remote_copy(
        src_ref=src,
        dst_ref=dst,
        send_sem=send_sem,
        recv_sem=recv_sem,
        device_id={axis: peer},
        device_id_type=MESH,
    )


def fold(x):
    rows, columns = x.shape
    y = jnp.sum(x.reshape(rows // 8, 8, columns), axis=0)
    out = y[:, :128]
    for at in range(128, columns, 128):
        out = out + y[:, at : at + 128]
    return out


def kernel(
    dims,
    table, weight, tiles, gtiles, price, flow, gen, ramp, demand, cost, gcap, rcap, fcap,
    o_gen, o_flow, o_price, o_ramp,
    tiles_v, a_v, price_v, flow_v, gen_v, ramp_v, demand_v, cost_v, gcap_v, rcap_v, fcap_v,
    pt_v, own_v, price1_v, flow_s, gen_s, dual_s, genlow_v,
    part_send, part_recv, fw_own, fw_in, d_send, d_recv, b_send, b_recv,
    ar1_s, ar1_r, ar2_s, ar2_r,
    og_v, of_v, op_v, or_v,
    in_sem, out_sem, ps_sem, pr_sem, fs_sem, fr_sem, ds_sem, dr_sem, bs_sem, br_sem,
    a1s_sem, a1r_sem, a2s_sem, a2r_sem,
):
    nt, nr, scen, count_p, count_d = dims
    t = lax.axis_index("tm")
    r = lax.axis_index("region")
    n_tiles, blk, _ = tiles.shape
    n_gens = gtiles.shape[0]
    lines, cols = flow.shape
    buses = price.shape[0]
    lb, bb = lines // blk, buses // blk
    width = 3 * lb + n_gens
    nch = part_send.shape[2]
    cw = lines // nch
    gw = n_gens * blk

    barrier = pltpu.get_barrier_semaphore()
    for axis, me, n in (("region", r, nr), ("tm", t, nt)):
        for k in range(1, n):
            pl.semaphore_signal(
                barrier, inc=1, device_id={axis: lax.rem(me + k, n)}, device_id_type=MESH
            )

    loads = [
        pltpu.make_async_copy(src, dst, in_sem.at[i])
        for i, (src, dst) in enumerate(
            (
                (price, price_v),
                (tiles, tiles_v.at[pl.ds(0, n_tiles)]),
                (gtiles, tiles_v.at[pl.ds(n_tiles, n_gens)]),
                (ramp, ramp_v),
                (flow, flow_v),
                (gen, gen_v),
                (fcap, fcap_v),
                (cost, cost_v),
                (gcap, gcap_v),
                (rcap, rcap_v),
                (demand, demand_v),
            )
        )
    ]
    for c in loads:
        c.start()

    tiles_v[n_tiles + n_gens] = jnp.zeros((blk, blk), bf16)

    @pl.when(r == 0)
    def _():
        part_recv[:, 1] = jnp.zeros_like(part_recv[:, 1])
        fw_in[:, 0] = jnp.zeros_like(fw_in[:, 0])

    @pl.when(r == nr - 1)
    def _():
        part_recv[:, 0] = jnp.zeros_like(part_recv[:, 0])
        fw_in[:, 1] = jnp.zeros_like(fw_in[:, 1])

    has = (r > 0, r < nr - 1)
    peer = (jnp.maximum(r - 1, 0), jnp.minimum(r + 1, nr - 1))
    t_next, t_prev = lax.rem(t + 1, nt), lax.rem(t + nt - 1, nt)

    def part_copy(it, side, ch):
        return remote(
            part_send.at[it, side, ch], part_recv.at[it, side, ch],
            ps_sem.at[it, side, ch], pr_sem.at[it, side, ch], "region", peer[side],
        )

    def flow_copy(it, side, ch):
        return remote(
            fw_own.at[it, ch], fw_in.at[it, 1 - side, ch],
            fs_sem.at[it, side, ch], fr_sem.at[it, 1 - side, ch], "region", peer[side],
        )

    def dual_copy(it):
        return remote(d_send.at[it], d_recv.at[it], ds_sem.at[it], dr_sem.at[it], "tm", t_prev)

    def bar_copy(it):
        return remote(b_send.at[it], b_recv.at[it], bs_sem.at[it], br_sem.at[it], "tm", t_next)

    side_at = (0, 2 * lines)

    def build(first, count):
        for w in range(first, first + count):
            for b in range(bb):
                a_v[b * blk : (b + 1) * blk, w * blk : (w + 1) * blk] = tiles_v[table[b * width + w]]

    def pull_out(it, start_hook=None):
        for ch in range(nch):
            for side in (0, 1):
                at = side_at[side] + ch * cw
                part_send[it, side, ch] = jnp.dot(
                    pt_v[...], a_v[:, at : at + cw], preferred_element_type=f32
                )
                if start_hook is not None and ch == 0 and side == 0:
                    start_hook()

                @pl.when(has[side])
                def _():
                    part_copy(it, side, ch).start()

    def pull_own():
        own_v[:, :lines] = jnp.dot(
            pt_v[...], a_v[:, lines : 2 * lines], preferred_element_type=f32
        )
        own_v[:, lines:] = jnp.dot(
            pt_v[...], a_v[:, 3 * lines :], preferred_element_type=f32
        )

    def set_pt(ref):
        for b in range(bb):
            pt_v[:, b * blk : (b + 1) * blk] = ref[b * blk : (b + 1) * blk, :].T.astype(bf16)

    def row(ref, n):
        return jnp.concatenate([ref[i : i + 1, :] for i in range(n)], axis=1) if n > 1 else ref[...]

    def primal(it, sp):
        acc = jnp.zeros((8, 128), f32)
        per = cw // blk
        for ch in range(nch):
            for side in (0, 1):
                @pl.when(has[1 - side])
                def _():
                    part_copy(it, side, ch).wait_recv()

            lo = ch * cw
            total = own_v[:, lo : lo + cw] + part_recv[it, 0, ch] + part_recv[it, 1, ch]
            cap = jnp.concatenate(
                [fcap_v[ch * per + i : ch * per + i + 1, :] for i in range(per)], axis=1
            )
            now = flow_s[it, :, lo : lo + cw]
            new = jnp.minimum(jnp.maximum(now + sp * total, -cap), cap)
            fw_own[it, ch] = (2.0 * new - now).astype(bf16)
            for side in (0, 1):
                @pl.when(has[side])
                def _():
                    flow_copy(it, side, ch).start()
            flow_s[it + 1, :, lo : lo + cw] = new
            if it == 0:
                acc = acc + fold((new - now) ** 2)
        dual_copy(it).wait_recv()
        dual = dual_s[it]
        nxt = d_recv[it]
        later = nxt if cols == scen else jnp.concatenate([dual[scen:], nxt], axis=0)
        gnow = gen_s[it]
        grad = row(cost_v, n_gens) - own_v[:, lines:] + (dual - later)
        gnew = jnp.minimum(jnp.maximum(gnow - sp * grad, 0.0), row(gcap_v, n_gens))
        gbar = 2.0 * gnew - gnow
        b_send[it] = gbar[cols - scen :]
        bar_copy(it).start()
        gen_s[it + 1] = gnew
        genlow_v[...] = gbar.astype(bf16)
        if it == 0:
            acc = acc + fold((gnew - gnow) ** 2)
        return acc, gbar

    nt_dims = (((1,), (1,)), ((), ()))

    def push(it, finish):
        half = buses // 2
        op_v[...] = lax.dot_general(
            a_v[:, 3 * lines :], genlow_v[...], nt_dims, preferred_element_type=f32
        )
        for ch in range(nch):
            at = lines + ch * cw
            op_v[...] += lax.dot_general(
                a_v[:, at : at + cw], fw_own[it, ch], nt_dims, preferred_element_type=f32
            )
        for ch in range(nch):
            for side in (0, 1):
                @pl.when(has[side])
                def _():
                    flow_copy(it, 1 - side, ch).wait_recv()
            for side in (0, 1):
                at = side_at[side] + ch * cw
                op_v[...] += lax.dot_general(
                    a_v[:, at : at + cw], fw_in[it, side, ch], nt_dims, preferred_element_type=f32
                )

    def ramp_step(it, gbar, sd):
        bar_copy(it).wait_recv()
        prev = b_recv[it]
        earlier = prev if cols == scen else jnp.concatenate([prev, gbar[: cols - scen]], axis=0)
        dual = dual_s[it]
        lifted = dual + sd * (gbar - earlier)
        bound = row(rcap_v, n_gens)
        return lifted - sd * jnp.minimum(jnp.maximum(lifted / sd, -bound), bound)

    w1 = jnp.full((1, 1), weight[0], f32)
    loads[0].wait()
    set_pt(price_v)
    loads[1].wait()
    loads[2].wait()
    build(0, lb)
    build(2 * lb, lb)
    loads[3].wait()
    dual_s[0] = ramp_v[...].T
    d_send[0] = dual_s[0][:scen]

    def entered():
        pl.semaphore_wait(barrier, nr - 1 + nt - 1)

    pull_out(0, entered)
    dual_copy(0).start()
    build(lb, lb)
    build(3 * lb, n_gens)
    pull_own()
    for c in loads[4:]:
        c.wait()
    for b in range(lb):
        flow_s[0, :, b * blk : (b + 1) * blk] = flow_v[b * blk : (b + 1) * blk, :].T
    gen_s[0] = gen_v[...].T
    sd1 = step_scale * w1
    primal_acc, gbar1 = primal(0, step_scale / w1)
    push(0, None)
    price_one = price_v[...] + sd1 * (demand_v[...] - op_v[...])
    price1_v[...] = price_one
    dual_acc = fold((price_one - price_v[...]) ** 2)
    dual_one = ramp_step(0, gbar1, sd1)
    dual_s[1] = dual_one
    dual_acc = dual_acc + fold((dual_one - dual_s[0]) ** 2)

    ar1_s[0] = primal_acc
    ar1_s[1] = dual_acc
    first = [
        remote(ar1_s, ar1_r.at[k], a1s_sem.at[k], a1r_sem.at[k], "tm", lax.rem(t + k, nt))
        for k in range(1, nt)
    ]
    for c in first:
        c.start()
    d_send[1] = dual_one[:scen]
    set_pt(price1_v)
    pull_out(1)
    dual_copy(1).start()
    for c in first:
        c.wait_recv()
    summed = ar1_s[...]
    for k in range(1, nt):
        summed = summed + ar1_r[k]
    ar2_s[...] = summed
    second = [
        remote(ar2_s, ar2_r.at[k], a2s_sem.at[k], a2r_sem.at[k], "region", lax.rem(r + k, nr))
        for k in range(1, nr)
    ]
    for c in second:
        c.start()
    pull_own()
    for c in second:
        c.wait_recv()
    summed = ar2_s[...]
    for k in range(1, nr):
        summed = summed + ar2_r[k]
    primal_mean = jnp.sum(summed[0], keepdims=True) / count_p
    dual_mean = jnp.sum(summed[1], keepdims=True) / count_d
    w2 = jnp.sqrt(w1 * jnp.sqrt((dual_mean + tiny) / (primal_mean + tiny)))

    sd2 = step_scale * w2
    _, gbar2 = primal(1, step_scale / w2)
    for b in range(lb):
        of_v[b * blk : (b + 1) * blk, :] = flow_s[2, :, b * blk : (b + 1) * blk].T
    og_v[...] = gen_s[2].T
    outs = [
        pltpu.make_async_copy(src, dst, out_sem.at[i])
        for i, (src, dst) in enumerate(
            ((of_v, o_flow), (og_v, o_gen), (or_v, o_ramp), (price_v, o_price))
        )
    ]
    outs[0].start()
    outs[1].start()
    push(1, None)
    price_v[...] = price1_v[...] + sd2 * (demand_v[...] - op_v[...])
    outs[3].start()
    or_v[...] = ramp_step(1, gbar2, sd2).T
    outs[2].start()

    for it in range(2):
        for ch in range(nch):
            for side in (0, 1):
                @pl.when(has[side])
                def _():
                    part_copy(it, side, ch).wait_send()
                    flow_copy(it, side, ch).wait_send()
        dual_copy(it).wait_send()
        bar_copy(it).wait_send()
    for c in first + second:
        c.wait_send()
    for c in outs:
        c.wait()


def shards(
    gen, flow, price, ramp_dual, demand, incid_tiles, tile_bus, tile_line, gen_tiles, gen_bus,
    gen_cost, gen_cap, ramp_cap, flow_cap, weight,
):
    gb, blk, hours, scen = gen.shape
    lb, bb = flow.shape[0], price.shape[0]
    n_tiles = incid_tiles.shape[0]
    cols = hours * scen
    nt, nr = lax.axis_size("tm"), lax.axis_size("region")
    region = lax.axis_index("region")
    lines, buses, gens = lb * blk, bb * blk, gb * blk
    width = 3 * lb + gb
    nch = 2 if lb % 2 == 0 else 1
    cw = lines // nch

    zero_at = n_tiles + gb
    slot = tile_bus * width + (tile_line - (region - 1) * lb)
    gslot = gen_bus * width + 3 * lb + jnp.arange(gb, dtype=jnp.int32)
    places = jnp.arange(bb * width, dtype=jnp.int32)[:, None]
    ids = jnp.arange(n_tiles, dtype=jnp.int32)
    gids = n_tiles + jnp.arange(gb, dtype=jnp.int32)
    table = (
        zero_at
        + jnp.sum(jnp.where(slot == places, ids - zero_at, 0), axis=1)
        + jnp.sum(jnp.where(gslot == places, gids - zero_at, 0), axis=1)
    ).astype(jnp.int32)

    dims = (
        nt, nr, scen,
        float((gen.size + flow.size) * nt * nr), float((price.size + ramp_dual.size) * nt * nr),
    )
    any_spec = pl.BlockSpec(memory_space=pl.ANY)
    smem_spec = pl.BlockSpec(memory_space=pltpu.SMEM)
    dma = pltpu.SemaphoreType.DMA
    V = pltpu.VMEM
    scratch = [
        V((n_tiles + gb + 1, blk, blk), bf16),
        V((buses, width * blk), bf16),
        V((buses, cols), f32),
        V((lines, cols), f32),
        V((gens, cols), f32),
        V((gens, cols), f32),
        V((buses, cols), f32),
        V((gb, blk), f32),
        V((gb, blk), f32),
        V((gb, blk), f32),
        V((lb, blk), f32),
        V((cols, buses), bf16),
        V((cols, lines + gens), f32),
        V((buses, cols), f32),
        V((3, cols, lines), f32),
        V((3, cols, gens), f32),
        V((2, cols, gens), f32),
        V((cols, gens), bf16),
        V((2, 2, nch, cols, cw), f32),
        V((2, 2, nch, cols, cw), f32),
        V((2, nch, cols, cw), bf16),
        V((2, 2, nch, cols, cw), bf16),
        V((2, scen, gens), f32),
        V((2, scen, gens), f32),
        V((2, scen, gens), f32),
        V((2, scen, gens), f32),
        V((2, 8, 128), f32),
        V((nt, 2, 8, 128), f32),
        V((2, 8, 128), f32),
        V((nr, 2, 8, 128), f32),
        V((gens, cols), f32),
        V((lines, cols), f32),
        V((buses, cols), f32),
        V((gens, cols), f32),
        dma((11,)),
        dma((4,)),
        dma((2, 2, nch)),
        dma((2, 2, nch)),
        dma((2, 2, nch)),
        dma((2, 2, nch)),
        dma((2,)),
        dma((2,)),
        dma((2,)),
        dma((2,)),
        dma((nt,)),
        dma((nt,)),
        dma((nr,)),
        dma((nr,)),
    ]
    outs = pl.pallas_call(
        functools.partial(kernel, dims),
        out_shape=(
            jax.ShapeDtypeStruct((gens, cols), f32),
            jax.ShapeDtypeStruct((lines, cols), f32),
            jax.ShapeDtypeStruct((buses, cols), f32),
            jax.ShapeDtypeStruct((gens, cols), f32),
        ),
        in_specs=[smem_spec, smem_spec] + [any_spec] * 11,
        out_specs=(any_spec,) * 4,
        scratch_shapes=scratch,
        compiler_params=pltpu.CompilerParams(collective_id=0, has_side_effects=True),
    )(
        table, weight.reshape(1), incid_tiles, gen_tiles,
        price.reshape(buses, cols), flow.reshape(lines, cols), gen.reshape(gens, cols),
        ramp_dual.reshape(gens, cols), demand.reshape(buses, cols),
        gen_cost, gen_cap, ramp_cap, flow_cap,
    )
    return tuple(
        out.reshape(like.shape) for out, like in zip(outs, (gen, flow, price, ramp_dual))
    )


def solution(mesh):
    field = P("region", None, "tm", None)
    placed = (
        field, field, field, field, field,
        P("region", None, None), P("region"), P("region"), P("region", None, None), P("region"),
        P("region", None), P("region", None), P("region", None), P("region", None), P(),
    )
    return jax.shard_map(
        shards, mesh=mesh, in_specs=placed, out_specs=(field,) * 4, check_vma=False
    )
```

```python
import functools

import jax
import jax.numpy as jnp
from jax import lax
from jax.experimental import pallas as pl
from jax.experimental.pallas import tpu as pltpu
from jax.sharding import PartitionSpec as P

MESH = pl.DeviceIdType.MESH
step_scale = 0.4
tiny = 1e-06
f32 = jnp.float32
bf16 = jnp.bfloat16


def remote(src, dst, send_sem, recv_sem, axis, peer):
    return pltpu.make_async_remote_copy(
        src_ref=src,
        dst_ref=dst,
        send_sem=send_sem,
        recv_sem=recv_sem,
        device_id={axis: peer},
        device_id_type=MESH,
    )


def fold(x):
    rows, columns = x.shape
    y = jnp.sum(x.reshape(rows // 8, 8, columns), axis=0)
    out = y[:, :128]
    for at in range(128, columns, 128):
        out = out + y[:, at : at + 128]
    return out


def both_halves(x):
    row = jnp.sum(x, axis=0, keepdims=True)
    return row + pltpu.roll(row, 64, 1)


def writer(*refs):
    n = (len(refs) - 1) // 2
    copies = [pltpu.make_async_copy(refs[i], refs[n + i], refs[-1].at[i]) for i in range(n)]
    for c in copies:
        c.start()
    for c in copies:
        c.wait()


def kernel(
    dims,
    table, weight, tiles, gtiles, price, flow, gen, ramp, demand, cost, gcap, rcap, fcap,
    o_gen, o_flow, o_price, o_ramp,
    tiles_v, a_v, price_v, flow_v, gen_v, ramp_v, demand_v, cost_v, gcap_v, rcap_v, fcap_v,
    pt_v, own_v, price1_v, flow_s, gen_s, dual_s, genlow_v,
    part_send, part_recv, fw_own, fw_in, d_send, d_recv, b_send, b_recv,
    ar_s, ar_r, acc_v,
    in_sem, ps_sem, pr_sem, fs_sem, fr_sem, ds_sem, dr_sem, bs_sem, br_sem,
    as_sem, ar_sem, ready,
):
    nt, nr, scen, count_p, count_d = dims
    t = lax.axis_index("tm")
    r = lax.axis_index("region")
    n_tiles, blk, _ = tiles.shape
    n_gens = gtiles.shape[0]
    lines, cols = flow.shape
    buses = price.shape[0]
    lb, bb = lines // blk, buses // blk
    width = 3 * lb + n_gens
    nch = part_send.shape[2]
    cw = lines // nch
    gw = n_gens * blk

    barrier = pltpu.get_barrier_semaphore()
    for axis, me, n in (("region", r, nr), ("tm", t, nt)):
        for k in range(1, n):
            pl.semaphore_signal(
                barrier, inc=1, device_id={axis: lax.rem(me + k, n)}, device_id_type=MESH
            )

    loads = [
        pltpu.make_async_copy(src, dst, in_sem.at[i])
        for i, (src, dst) in enumerate(
            (
                (price, price_v),
                (tiles, tiles_v.at[pl.ds(0, n_tiles)]),
                (gtiles, tiles_v.at[pl.ds(n_tiles, n_gens)]),
                (ramp, ramp_v),
                (flow, flow_v),
                (gen, gen_v),
                (fcap, fcap_v),
                (cost, cost_v),
                (gcap, gcap_v),
                (rcap, rcap_v),
                (demand, demand_v),
            )
        )
    ]
    for c in loads:
        c.start()

    tiles_v[n_tiles + n_gens] = jnp.zeros((blk, blk), bf16)

    @pl.when(r == 0)
    def _():
        part_recv[:, 1] = jnp.zeros_like(part_recv[:, 1])
        fw_in[:, 0] = jnp.zeros_like(fw_in[:, 0])

    @pl.when(r == nr - 1)
    def _():
        part_recv[:, 0] = jnp.zeros_like(part_recv[:, 0])
        fw_in[:, 1] = jnp.zeros_like(fw_in[:, 1])

    has = (r > 0, r < nr - 1)
    peer = (jnp.maximum(r - 1, 0), jnp.minimum(r + 1, nr - 1))
    t_next, t_prev = lax.rem(t + 1, nt), lax.rem(t + nt - 1, nt)

    def part_copy(it, side, ch):
        return remote(
            part_send.at[it, side, ch], part_recv.at[it, side, ch],
            ps_sem.at[it, side, ch], pr_sem.at[it, side, ch], "region", peer[side],
        )

    def flow_copy(it, side, ch):
        return remote(
            fw_own.at[it, ch], fw_in.at[it, 1 - side, ch],
            fs_sem.at[it, side, ch], fr_sem.at[it, 1 - side, ch], "region", peer[side],
        )

    def dual_copy(it):
        return remote(d_send.at[it], d_recv.at[it], ds_sem.at[it], dr_sem.at[it], "tm", t_prev)

    def bar_copy(it):
        return remote(b_send.at[it], b_recv.at[it], bs_sem.at[it], br_sem.at[it], "tm", t_next)

    side_at = (0, 2 * lines)

    def build(first, count):
        for w in range(first, first + count):
            for b in range(bb):
                a_v[b * blk : (b + 1) * blk, w * blk : (w + 1) * blk] = tiles_v[table[b * width + w]]

    def pull_out(it, start_hook=None):
        for ch in range(nch):
            for side in (0, 1):
                at = side_at[side] + ch * cw
                part_send[it, side, ch] = jnp.dot(
                    pt_v[...], a_v[:, at : at + cw], preferred_element_type=f32
                )
                if start_hook is not None and ch == 0 and side == 0:
                    start_hook()

                @pl.when(has[side])
                def _():
                    part_copy(it, side, ch).start()

    def pull_own():
        own_v[:, :lines] = jnp.dot(
            pt_v[...], a_v[:, lines : 2 * lines], preferred_element_type=f32
        )
        own_v[:, lines:] = jnp.dot(
            pt_v[...], a_v[:, 3 * lines :], preferred_element_type=f32
        )

    def set_pt(ref):
        for b in range(bb):
            pt_v[:, b * blk : (b + 1) * blk] = ref[b * blk : (b + 1) * blk, :].T.astype(bf16)

    def row(ref, n):
        return jnp.concatenate([ref[i : i + 1, :] for i in range(n)], axis=1) if n > 1 else ref[...]

    def primal(it, sp):
        acc = jnp.zeros((8, 128), f32)
        per = cw // blk
        for ch in range(nch):
            for side in (0, 1):
                @pl.when(has[1 - side])
                def _():
                    part_copy(it, side, ch).wait_recv()

            lo = ch * cw
            total = own_v[:, lo : lo + cw] + part_recv[it, 0, ch] + part_recv[it, 1, ch]
            cap = jnp.concatenate(
                [fcap_v[ch * per + i : ch * per + i + 1, :] for i in range(per)], axis=1
            )
            now = flow_s[it, :, lo : lo + cw]
            new = jnp.minimum(jnp.maximum(now + sp * total, -cap), cap)
            fw_own[it, ch] = (2.0 * new - now).astype(bf16)
            for side in (0, 1):
                @pl.when(has[side])
                def _():
                    flow_copy(it, side, ch).start()
            flow_s[it + 1, :, lo : lo + cw] = new
            if it == 0:
                acc = acc + fold((new - now) ** 2)
        dual_copy(it).wait_recv()
        dual = dual_s[it]
        nxt = d_recv[it]
        later = nxt if cols == scen else jnp.concatenate([dual[scen:], nxt], axis=0)
        gnow = gen_s[it]
        grad = row(cost_v, n_gens) - own_v[:, lines:] + (dual - later)
        gnew = jnp.minimum(jnp.maximum(gnow - sp * grad, 0.0), row(gcap_v, n_gens))
        gbar = 2.0 * gnew - gnow
        b_send[it] = gbar[cols - scen :]
        bar_copy(it).start()
        gen_s[it + 1] = gnew
        genlow_v[...] = gbar.astype(bf16)
        if it == 0:
            acc = acc + fold((gnew - gnow) ** 2)
        return acc, gbar

    nt_dims = (((1,), (1,)), ((), ()))

    def push(it, finish):
        half = buses // 2
        acc_v[...] = lax.dot_general(
            a_v[:, 3 * lines :], genlow_v[...], nt_dims, preferred_element_type=f32
        )
        for ch in range(nch):
            at = lines + ch * cw
            acc_v[...] += lax.dot_general(
                a_v[:, at : at + cw], fw_own[it, ch], nt_dims, preferred_element_type=f32
            )
        for ch in range(nch):
            for side in (0, 1):
                @pl.when(has[side])
                def _():
                    flow_copy(it, 1 - side, ch).wait_recv()
            for side in (0, 1):
                at = side_at[side] + ch * cw
                acc_v[...] += lax.dot_general(
                    a_v[:, at : at + cw], fw_in[it, side, ch], nt_dims, preferred_element_type=f32
                )

    def ramp_step(it, gbar, sd):
        bar_copy(it).wait_recv()
        prev = b_recv[it]
        earlier = prev if cols == scen else jnp.concatenate([prev, gbar[: cols - scen]], axis=0)
        dual = dual_s[it]
        lifted = dual + sd * (gbar - earlier)
        bound = row(rcap_v, n_gens)
        return lifted - sd * jnp.minimum(jnp.maximum(lifted / sd, -bound), bound)

    w1 = jnp.full((1, 1), weight[0], f32)
    loads[0].wait()
    set_pt(price_v)
    loads[1].wait()
    loads[2].wait()
    build(0, lb)
    build(2 * lb, lb)
    loads[3].wait()
    dual_s[0] = ramp_v[...].T
    d_send[0] = dual_s[0][:scen]

    def entered():
        pl.semaphore_wait(barrier, nr - 1 + nt - 1)
        for k in range(1, nr):
            pl.semaphore_signal(
                ready, inc=1, device_id={"region": lax.rem(r + k, nr)}, device_id_type=MESH
            )

    pull_out(0, entered)
    dual_copy(0).start()
    build(lb, lb)
    build(3 * lb, n_gens)
    pull_own()
    for c in loads[4:]:
        c.wait()
    for b in range(lb):
        flow_s[0, :, b * blk : (b + 1) * blk] = flow_v[b * blk : (b + 1) * blk, :].T
    gen_s[0] = gen_v[...].T
    sd1 = step_scale * w1
    primal_acc, gbar1 = primal(0, step_scale / w1)
    push(0, None)
    price_one = price_v[...] + sd1 * (demand_v[...] - acc_v[...])
    price1_v[...] = price_one
    dual_acc = fold((price_one - price_v[...]) ** 2)
    dual_one = ramp_step(0, gbar1, sd1)
    dual_s[1] = dual_one
    dual_acc = dual_acc + fold((dual_one - dual_s[0]) ** 2)

    low = lax.broadcasted_iota(jnp.int32, (1, 128), 1) < 64
    ar_s[...] = jnp.where(low, both_halves(primal_acc), both_halves(dual_acc))
    sums = []
    for j in range(nt):
        for k in range(nr):
            if j or k:
                at = j * nr + k
                sums.append(
                    pltpu.make_async_remote_copy(
                        src_ref=ar_s,
                        dst_ref=ar_r.at[at],
                        send_sem=as_sem.at[at],
                        recv_sem=ar_sem.at[at],
                        device_id={"tm": lax.rem(t + j, nt), "region": lax.rem(r + k, nr)},
                        device_id_type=MESH,
                    )
                )
    pl.semaphore_wait(ready, nr - 1)
    for c in sums:
        c.start()
    d_send[1] = dual_one[:scen]
    set_pt(price1_v)
    pull_out(1)
    dual_copy(1).start()
    pull_own()
    for c in sums:
        c.wait_recv()
    summed = ar_s[...]
    for at in range(1, nt * nr):
        summed = summed + ar_r[at]
    primal_mean = jnp.sum(jnp.where(low, summed, 0.0), axis=1, keepdims=True) / count_p
    dual_mean = jnp.sum(jnp.where(low, 0.0, summed), axis=1, keepdims=True) / count_d
    w2 = jnp.sqrt(w1 * jnp.sqrt((dual_mean + tiny) / (primal_mean + tiny)))

    sd2 = step_scale * w2
    _, gbar2 = primal(1, step_scale / w2)
    for b in range(lb):
        o_flow[b * blk : (b + 1) * blk, :] = flow_s[2, :, b * blk : (b + 1) * blk].T
    o_gen[...] = gen_s[2].T
    push(1, None)
    o_price[...] = price1_v[...] + sd2 * (demand_v[...] - acc_v[...])
    o_ramp[...] = ramp_step(1, gbar2, sd2).T

    for it in range(2):
        for ch in range(nch):
            for side in (0, 1):
                @pl.when(has[side])
                def _():
                    part_copy(it, side, ch).wait_send()
                    flow_copy(it, side, ch).wait_send()
        dual_copy(it).wait_send()
        bar_copy(it).wait_send()
    for c in sums:
        c.wait_send()


def shards(
    gen, flow, price, ramp_dual, demand, incid_tiles, tile_bus, tile_line, gen_tiles, gen_bus,
    gen_cost, gen_cap, ramp_cap, flow_cap, weight,
):
    gb, blk, hours, scen = gen.shape
    lb, bb = flow.shape[0], price.shape[0]
    n_tiles = incid_tiles.shape[0]
    cols = hours * scen
    nt, nr = lax.axis_size("tm"), lax.axis_size("region")
    region = lax.axis_index("region")
    lines, buses, gens = lb * blk, bb * blk, gb * blk
    width = 3 * lb + gb
    nch = 2 if lb % 2 == 0 else 1
    cw = lines // nch

    zero_at = n_tiles + gb
    slot = tile_bus * width + (tile_line - (region - 1) * lb)
    gslot = gen_bus * width + 3 * lb + jnp.arange(gb, dtype=jnp.int32)
    places = jnp.arange(bb * width, dtype=jnp.int32)[:, None]
    ids = jnp.arange(n_tiles, dtype=jnp.int32)
    gids = n_tiles + jnp.arange(gb, dtype=jnp.int32)
    table = jnp.clip(
        zero_at
        + jnp.sum(jnp.where(slot == places, ids - zero_at, 0), axis=1)
        + jnp.sum(jnp.where(gslot == places, gids - zero_at, 0), axis=1),
        0,
        zero_at,
    ).astype(jnp.int32)

    dims = (
        nt, nr, scen,
        float((gen.size + flow.size) * nt * nr), float((price.size + ramp_dual.size) * nt * nr),
    )
    any_spec = pl.BlockSpec(memory_space=pl.ANY)
    smem_spec = pl.BlockSpec(memory_space=pltpu.SMEM)
    dma = pltpu.SemaphoreType.DMA
    V = pltpu.VMEM
    scratch = [
        V((n_tiles + gb + 1, blk, blk), bf16),
        V((buses, width * blk), bf16),
        V((buses, cols), f32),
        V((lines, cols), f32),
        V((gens, cols), f32),
        V((gens, cols), f32),
        V((buses, cols), f32),
        V((gb, blk), f32),
        V((gb, blk), f32),
        V((gb, blk), f32),
        V((lb, blk), f32),
        V((cols, buses), bf16),
        V((cols, lines + gens), f32),
        V((buses, cols), f32),
        V((3, cols, lines), f32),
        V((3, cols, gens), f32),
        V((2, cols, gens), f32),
        V((cols, gens), bf16),
        V((2, 2, nch, cols, cw), f32),
        V((2, 2, nch, cols, cw), f32),
        V((2, nch, cols, cw), bf16),
        V((2, 2, nch, cols, cw), bf16),
        V((2, scen, gens), f32),
        V((2, scen, gens), f32),
        V((2, scen, gens), f32),
        V((2, scen, gens), f32),
        V((1, 128), f32),
        V((nt * nr, 1, 128), f32),
        V((buses, cols), f32),
        dma((11,)),
        dma((2, 2, nch)),
        dma((2, 2, nch)),
        dma((2, 2, nch)),
        dma((2, 2, nch)),
        dma((2,)),
        dma((2,)),
        dma((2,)),
        dma((2,)),
        dma((nt * nr,)),
        dma((nt * nr,)),
        pltpu.SemaphoreType.REGULAR,
    ]
    vmem_spec = pl.BlockSpec(memory_space=pltpu.VMEM)
    shapes = ((gens, cols), (lines, cols), (buses, cols), (gens, cols))
    outs = pl.pallas_call(
        functools.partial(kernel, dims),
        out_shape=tuple(V(shape, f32) for shape in shapes),
        in_specs=[smem_spec, smem_spec] + [any_spec] * 11,
        out_specs=(vmem_spec,) * 4,
        scratch_shapes=scratch,
        compiler_params=pltpu.CompilerParams(collective_id=0, has_side_effects=True),
    )(
        table, weight.reshape(1), incid_tiles, gen_tiles,
        price.reshape(buses, cols), flow.reshape(lines, cols), gen.reshape(gens, cols),
        ramp_dual.reshape(gens, cols), demand.reshape(buses, cols),
        gen_cost, gen_cap, ramp_cap, flow_cap,
    )
    outs = pl.pallas_call(
        writer,
        out_shape=tuple(jax.ShapeDtypeStruct(shape, f32) for shape in shapes),
        in_specs=[any_spec] * 4,
        out_specs=(any_spec,) * 4,
        scratch_shapes=[dma((4,))],
    )(*(pltpu.with_memory_space_constraint(out, pltpu.VMEM) for out in outs))
    return tuple(
        out.reshape(like.shape) for out, like in zip(outs, (gen, flow, price, ramp_dual))
    )


def solution(mesh):
    field = P("region", None, "tm", None)
    placed = (
        field, field, field, field, field,
        P("region", None, None), P("region"), P("region"), P("region", None, None), P("region"),
        P("region", None), P("region", None), P("region", None), P("region", None), P(),
    )
    return jax.shard_map(
        shards, mesh=mesh, in_specs=placed, out_specs=(field,) * 4, check_vma=False
    )
```

```python
import functools

import jax
import jax.numpy as jnp
from jax import lax
from jax.experimental import pallas as pl
from jax.experimental.pallas import tpu as pltpu
from jax.sharding import PartitionSpec as P

MESH = pl.DeviceIdType.MESH
step_scale = 0.4
tiny = 1e-06
f32 = jnp.float32
bf16 = jnp.bfloat16


def remote(src, dst, send_sem, recv_sem, axis, peer):
    return pltpu.make_async_remote_copy(
        src_ref=src,
        dst_ref=dst,
        send_sem=send_sem,
        recv_sem=recv_sem,
        device_id={axis: peer},
        device_id_type=MESH,
    )


def fold(x):
    rows, columns = x.shape
    y = jnp.sum(x.reshape(rows // 8, 8, columns), axis=0)
    out = y[:, :128]
    for at in range(128, columns, 128):
        out = out + y[:, at : at + 128]
    return out


def both_halves(x):
    row = jnp.sum(x, axis=0, keepdims=True)
    return row + pltpu.roll(row, 64, 1)


def writer(*refs):
    n = (len(refs) - 1) // 2
    copies = [pltpu.make_async_copy(refs[i], refs[n + i], refs[-1].at[i]) for i in range(n)]
    for c in copies:
        c.start()
    for c in copies:
        c.wait()


def kernel(
    dims,
    gen_bus, weight, tile_bus, tile_line, tiles, gtiles, price, flow, gen, ramp, demand, cost, gcap, rcap, fcap,
    o_gen, o_flow, o_price, o_ramp,
    tiles_v, a_v, price_v, flow_v, gen_v, ramp_v, demand_v, cost_v, gcap_v, rcap_v, fcap_v,
    pt_v, own_v, price1_v, flow_s, gen_s, dual_s, genlow_v,
    part_send, part_recv, fw_own, fw_in, d_send, d_recv, b_send, b_recv,
    ar_s, ar_r, acc_v, bus_v, line_v, table_v, table_s,
    in_sem, ps_sem, pr_sem, fs_sem, fr_sem, ds_sem, dr_sem, bs_sem, br_sem,
    as_sem, ar_sem, ready, table_sem,
):
    nt, nr, scen, count_p, count_d = dims
    t = lax.axis_index("tm")
    r = lax.axis_index("region")
    n_tiles, blk, _ = tiles.shape
    n_gens = gtiles.shape[0]
    lines, cols = flow.shape
    buses = price.shape[0]
    lb, bb = lines // blk, buses // blk
    width = 3 * lb + n_gens
    nch = part_send.shape[2]
    cw = lines // nch
    gw = n_gens * blk

    barrier = pltpu.get_barrier_semaphore()
    for axis, me, n in (("region", r, nr), ("tm", t, nt)):
        for k in range(1, n):
            pl.semaphore_signal(
                barrier, inc=1, device_id={axis: lax.rem(me + k, n)}, device_id_type=MESH
            )

    loads = [
        pltpu.make_async_copy(src, dst, in_sem.at[i])
        for i, (src, dst) in enumerate(
            (
                (tile_bus, bus_v),
                (tile_line, line_v),
                (price, price_v),
                (tiles, tiles_v.at[pl.ds(0, n_tiles)]),
                (gtiles, tiles_v.at[pl.ds(n_tiles, n_gens)]),
                (ramp, ramp_v),
                (flow, flow_v),
                (gen, gen_v),
                (fcap, fcap_v),
                (cost, cost_v),
                (gcap, gcap_v),
                (rcap, rcap_v),
                (demand, demand_v),
            )
        )
    ]
    for c in loads:
        c.start()

    tiles_v[n_tiles + n_gens] = jnp.zeros((blk, blk), bf16)

    @pl.when(r == 0)
    def _():
        part_recv[:, 1] = jnp.zeros_like(part_recv[:, 1])
        fw_in[:, 0] = jnp.zeros_like(fw_in[:, 0])

    @pl.when(r == nr - 1)
    def _():
        part_recv[:, 0] = jnp.zeros_like(part_recv[:, 0])
        fw_in[:, 1] = jnp.zeros_like(fw_in[:, 1])

    has = (r > 0, r < nr - 1)
    peer = (jnp.maximum(r - 1, 0), jnp.minimum(r + 1, nr - 1))
    t_next, t_prev = lax.rem(t + 1, nt), lax.rem(t + nt - 1, nt)

    def part_copy(it, side, ch):
        return remote(
            part_send.at[it, side, ch], part_recv.at[it, side, ch],
            ps_sem.at[it, side, ch], pr_sem.at[it, side, ch], "region", peer[side],
        )

    def flow_copy(it, side, ch):
        return remote(
            fw_own.at[it, ch], fw_in.at[it, 1 - side, ch],
            fs_sem.at[it, side, ch], fr_sem.at[it, 1 - side, ch], "region", peer[side],
        )

    def dual_copy(it):
        return remote(d_send.at[it], d_recv.at[it], ds_sem.at[it], dr_sem.at[it], "tm", t_prev)

    def bar_copy(it):
        return remote(b_send.at[it], b_recv.at[it], bs_sem.at[it], br_sem.at[it], "tm", t_next)

    side_at = (0, 2 * lines)

    def build(first, count):
        for w in range(first, first + count):
            for b in range(bb):
                a_v[b * blk : (b + 1) * blk, w * blk : (w + 1) * blk] = tiles_v[table_s[0, b * width + w]]

    def pull_out(it, start_hook=None):
        for ch in range(nch):
            for side in (0, 1):
                at = side_at[side] + ch * cw
                part_send[it, side, ch] = jnp.dot(
                    pt_v[...], a_v[:, at : at + cw], preferred_element_type=f32
                )
                if start_hook is not None and ch == 0 and side == 0:
                    start_hook()

                @pl.when(has[side])
                def _():
                    part_copy(it, side, ch).start()

    def pull_own():
        own_v[:, :lines] = jnp.dot(
            pt_v[...], a_v[:, lines : 2 * lines], preferred_element_type=f32
        )
        own_v[:, lines:] = jnp.dot(
            pt_v[...], a_v[:, 3 * lines :], preferred_element_type=f32
        )

    def set_pt(ref):
        for b in range(bb):
            pt_v[:, b * blk : (b + 1) * blk] = ref[b * blk : (b + 1) * blk, :].T.astype(bf16)

    def row(ref, n):
        return jnp.concatenate([ref[i : i + 1, :] for i in range(n)], axis=1) if n > 1 else ref[...]

    def primal(it, sp):
        acc = jnp.zeros((8, 128), f32)
        per = cw // blk
        for ch in range(nch):
            for side in (0, 1):
                @pl.when(has[1 - side])
                def _():
                    part_copy(it, side, ch).wait_recv()

            lo = ch * cw
            total = own_v[:, lo : lo + cw] + part_recv[it, 0, ch] + part_recv[it, 1, ch]
            cap = jnp.concatenate(
                [fcap_v[ch * per + i : ch * per + i + 1, :] for i in range(per)], axis=1
            )
            now = flow_s[it, :, lo : lo + cw]
            new = jnp.minimum(jnp.maximum(now + sp * total, -cap), cap)
            fw_own[it, ch] = (2.0 * new - now).astype(bf16)
            for side in (0, 1):
                @pl.when(has[side])
                def _():
                    flow_copy(it, side, ch).start()
            flow_s[it + 1, :, lo : lo + cw] = new
            if it == 0:
                acc = acc + fold((new - now) ** 2)
        dual_copy(it).wait_recv()
        dual = dual_s[it]
        nxt = d_recv[it]
        later = nxt if cols == scen else jnp.concatenate([dual[scen:], nxt], axis=0)
        gnow = gen_s[it]
        grad = row(cost_v, n_gens) - own_v[:, lines:] + (dual - later)
        gnew = jnp.minimum(jnp.maximum(gnow - sp * grad, 0.0), row(gcap_v, n_gens))
        gbar = 2.0 * gnew - gnow
        b_send[it] = gbar[cols - scen :]
        bar_copy(it).start()
        gen_s[it + 1] = gnew
        genlow_v[...] = gbar.astype(bf16)
        if it == 0:
            acc = acc + fold((gnew - gnow) ** 2)
        return acc, gbar

    nt_dims = (((1,), (1,)), ((), ()))

    def push(it, finish):
        half = buses // 2
        acc_v[...] = lax.dot_general(
            a_v[:, 3 * lines :], genlow_v[...], nt_dims, preferred_element_type=f32
        )
        for ch in range(nch):
            at = lines + ch * cw
            acc_v[...] += lax.dot_general(
                a_v[:, at : at + cw], fw_own[it, ch], nt_dims, preferred_element_type=f32
            )
        for ch in range(nch):
            for side in (0, 1):
                @pl.when(has[side])
                def _():
                    flow_copy(it, 1 - side, ch).wait_recv()
            for side in (0, 1):
                at = side_at[side] + ch * cw
                acc_v[...] += lax.dot_general(
                    a_v[:, at : at + cw], fw_in[it, side, ch], nt_dims, preferred_element_type=f32
                )

    def ramp_step(it, gbar, sd):
        bar_copy(it).wait_recv()
        prev = b_recv[it]
        earlier = prev if cols == scen else jnp.concatenate([prev, gbar[: cols - scen]], axis=0)
        dual = dual_s[it]
        lifted = dual + sd * (gbar - earlier)
        bound = row(rcap_v, n_gens)
        return lifted - sd * jnp.minimum(jnp.maximum(lifted / sd, -bound), bound)

    zero_at = n_tiles + n_gens
    loads[0].wait()
    loads[1].wait()
    slot = bus_v[...] * width + (line_v[...] - (r - 1) * lb)
    down = lax.broadcasted_iota(jnp.int32, (n_tiles, n_tiles), 0)
    across = lax.broadcasted_iota(jnp.int32, (n_tiles, n_tiles), 1)
    upright = jnp.sum(jnp.where(down == across, slot, 0), axis=1, keepdims=True)
    places = lax.broadcasted_iota(jnp.int32, (n_tiles, 128), 1)
    ids = lax.broadcasted_iota(jnp.int32, (n_tiles, 128), 0)
    found = jnp.sum(jnp.where(upright == places, ids - zero_at, 0), axis=0, keepdims=True)
    lane = lax.broadcasted_iota(jnp.int32, (1, 128), 1)
    for g in range(n_gens):
        found = jnp.where(lane == gen_bus[g] * width + 3 * lb + g, n_tiles + g - zero_at, found)
    table_v[...] = jnp.clip(zero_at + found, 0, zero_at)
    to_scalar = pltpu.make_async_copy(table_v, table_s, table_sem.at[0])
    to_scalar.start()

    w1 = jnp.full((1, 1), weight[0], f32)
    loads[2].wait()
    set_pt(price_v)
    loads[3].wait()
    loads[4].wait()
    to_scalar.wait()
    build(0, lb)
    build(2 * lb, lb)
    loads[5].wait()
    dual_s[0] = ramp_v[...].T
    d_send[0] = dual_s[0][:scen]

    def entered():
        pl.semaphore_wait(barrier, nr - 1 + nt - 1)
        for k in range(1, nr):
            pl.semaphore_signal(
                ready, inc=1, device_id={"region": lax.rem(r + k, nr)}, device_id_type=MESH
            )

    pull_out(0, entered)
    dual_copy(0).start()
    build(lb, lb)
    build(3 * lb, n_gens)
    pull_own()
    for c in loads[6:]:
        c.wait()
    for b in range(lb):
        flow_s[0, :, b * blk : (b + 1) * blk] = flow_v[b * blk : (b + 1) * blk, :].T
    gen_s[0] = gen_v[...].T
    sd1 = step_scale * w1
    primal_acc, gbar1 = primal(0, step_scale / w1)
    push(0, None)
    price_one = price_v[...] + sd1 * (demand_v[...] - acc_v[...])
    price1_v[...] = price_one
    dual_acc = fold((price_one - price_v[...]) ** 2)
    dual_one = ramp_step(0, gbar1, sd1)
    dual_s[1] = dual_one
    dual_acc = dual_acc + fold((dual_one - dual_s[0]) ** 2)

    low = lax.broadcasted_iota(jnp.int32, (1, 128), 1) < 64
    ar_s[...] = jnp.where(low, both_halves(primal_acc), both_halves(dual_acc))
    sums = []
    for j in range(nt):
        for k in range(nr):
            if j or k:
                at = j * nr + k
                sums.append(
                    pltpu.make_async_remote_copy(
                        src_ref=ar_s,
                        dst_ref=ar_r.at[at],
                        send_sem=as_sem.at[at],
                        recv_sem=ar_sem.at[at],
                        device_id={"tm": lax.rem(t + j, nt), "region": lax.rem(r + k, nr)},
                        device_id_type=MESH,
                    )
                )
    pl.semaphore_wait(ready, nr - 1)
    for c in sums:
        c.start()
    d_send[1] = dual_one[:scen]
    set_pt(price1_v)
    pull_out(1)
    dual_copy(1).start()
    pull_own()
    for c in sums:
        c.wait_recv()
    summed = ar_s[...]
    for at in range(1, nt * nr):
        summed = summed + ar_r[at]
    primal_mean = jnp.sum(jnp.where(low, summed, 0.0), axis=1, keepdims=True) / count_p
    dual_mean = jnp.sum(jnp.where(low, 0.0, summed), axis=1, keepdims=True) / count_d
    w2 = jnp.sqrt(w1 * jnp.sqrt((dual_mean + tiny) / (primal_mean + tiny)))

    sd2 = step_scale * w2
    _, gbar2 = primal(1, step_scale / w2)
    for b in range(lb):
        o_flow[b * blk : (b + 1) * blk, :] = flow_s[2, :, b * blk : (b + 1) * blk].T
    o_gen[...] = gen_s[2].T
    push(1, None)
    o_price[...] = price1_v[...] + sd2 * (demand_v[...] - acc_v[...])
    o_ramp[...] = ramp_step(1, gbar2, sd2).T

    for it in range(2):
        for ch in range(nch):
            for side in (0, 1):
                @pl.when(has[side])
                def _():
                    part_copy(it, side, ch).wait_send()
                    flow_copy(it, side, ch).wait_send()
        dual_copy(it).wait_send()
        bar_copy(it).wait_send()
    for c in sums:
        c.wait_send()


def shards(
    gen, flow, price, ramp_dual, demand, incid_tiles, tile_bus, tile_line, gen_tiles, gen_bus,
    gen_cost, gen_cap, ramp_cap, flow_cap, weight,
):
    gb, blk, hours, scen = gen.shape
    lb, bb = flow.shape[0], price.shape[0]
    n_tiles = incid_tiles.shape[0]
    cols = hours * scen
    nt, nr = lax.axis_size("tm"), lax.axis_size("region")
    lines, buses, gens = lb * blk, bb * blk, gb * blk
    width = 3 * lb + gb
    nch = 2 if lb % 2 == 0 else 1
    cw = lines // nch

    dims = (
        nt, nr, scen,
        float((gen.size + flow.size) * nt * nr), float((price.size + ramp_dual.size) * nt * nr),
    )
    any_spec = pl.BlockSpec(memory_space=pl.ANY)
    smem_spec = pl.BlockSpec(memory_space=pltpu.SMEM)
    dma = pltpu.SemaphoreType.DMA
    V = pltpu.VMEM
    scratch = [
        V((n_tiles + gb + 1, blk, blk), bf16),
        V((buses, width * blk), bf16),
        V((buses, cols), f32),
        V((lines, cols), f32),
        V((gens, cols), f32),
        V((gens, cols), f32),
        V((buses, cols), f32),
        V((gb, blk), f32),
        V((gb, blk), f32),
        V((gb, blk), f32),
        V((lb, blk), f32),
        V((cols, buses), bf16),
        V((cols, lines + gens), f32),
        V((buses, cols), f32),
        V((3, cols, lines), f32),
        V((3, cols, gens), f32),
        V((2, cols, gens), f32),
        V((cols, gens), bf16),
        V((2, 2, nch, cols, cw), f32),
        V((2, 2, nch, cols, cw), f32),
        V((2, nch, cols, cw), bf16),
        V((2, 2, nch, cols, cw), bf16),
        V((2, scen, gens), f32),
        V((2, scen, gens), f32),
        V((2, scen, gens), f32),
        V((2, scen, gens), f32),
        V((1, 128), f32),
        V((nt * nr, 1, 128), f32),
        V((buses, cols), f32),
        V((1, n_tiles), jnp.int32),
        V((1, n_tiles), jnp.int32),
        V((1, 128), jnp.int32),
        pltpu.SMEM((1, 128), jnp.int32),
        dma((13,)),
        dma((2, 2, nch)),
        dma((2, 2, nch)),
        dma((2, 2, nch)),
        dma((2, 2, nch)),
        dma((2,)),
        dma((2,)),
        dma((2,)),
        dma((2,)),
        dma((nt * nr,)),
        dma((nt * nr,)),
        pltpu.SemaphoreType.REGULAR,
        dma((1,)),
    ]
    vmem_spec = pl.BlockSpec(memory_space=pltpu.VMEM)
    shapes = ((gens, cols), (lines, cols), (buses, cols), (gens, cols))
    outs = pl.pallas_call(
        functools.partial(kernel, dims),
        out_shape=tuple(V(shape, f32) for shape in shapes),
        in_specs=[smem_spec, smem_spec] + [any_spec] * 13,
        out_specs=(vmem_spec,) * 4,
        scratch_shapes=scratch,
        compiler_params=pltpu.CompilerParams(collective_id=0, has_side_effects=True),
    )(
        gen_bus, weight.reshape(1), tile_bus.reshape(1, n_tiles), tile_line.reshape(1, n_tiles), incid_tiles, gen_tiles,
        price.reshape(buses, cols), flow.reshape(lines, cols), gen.reshape(gens, cols),
        ramp_dual.reshape(gens, cols), demand.reshape(buses, cols),
        gen_cost, gen_cap, ramp_cap, flow_cap,
    )
    outs = pl.pallas_call(
        writer,
        out_shape=tuple(jax.ShapeDtypeStruct(shape, f32) for shape in shapes),
        in_specs=[any_spec] * 4,
        out_specs=(any_spec,) * 4,
        scratch_shapes=[dma((4,))],
    )(*(pltpu.with_memory_space_constraint(out, pltpu.VMEM) for out in outs))
    return tuple(
        out.reshape(like.shape) for out, like in zip(outs, (gen, flow, price, ramp_dual))
    )


def solution(mesh):
    field = P("region", None, "tm", None)
    placed = (
        field, field, field, field, field,
        P("region", None, None), P("region"), P("region"), P("region", None, None), P("region"),
        P("region", None), P("region", None), P("region", None), P("region", None), P(),
    )
    return jax.shard_map(
        shards, mesh=mesh, in_specs=placed, out_specs=(field,) * 4, check_vma=False
    )
```
